32 devices in a mesh: gx: 8 (over z, core), gy: 4 (over y, x).
Axes of the slice: x: 2, y: 2, z: 4, core: 2. Of those that a mesh axis runs over, the one named last changes fastest.
Arguments:
- theta: float32 [32, 1024, 1024], P('gx', 'gy'), may hold values from 0.9 to 1.4
- pressure: float32 [32, 1024, 1024], P('gx', 'gy'), may hold values from 0.1 to 1
- vertical_wind: float32 [32, 1024, 1024], P('gx', 'gy'), may hold values from -6 to 6
- terrain: float32 [1024, 1024], P('gx', 'gy'), may hold values from 0 to 0.5
- column_mass: float32 [1024, 1024], P('gx', 'gy'), may hold values from 0.5 to 1
- land_mask: int32 [1024, 1024], P('gx', 'gy'), may hold values 0 or 1
- pbl_top: int32 [1024, 1024], P('gx', 'gy'), may hold values from 2 to 27
Outputs:
- updated_wind: float32 [32, 1024, 1024], P(None, 'gx', 'gy')
- geopotential: float32 [32, 1024, 1024], P(None, 'gx', 'gy')
The draws below stay inside these ranges and needn't reach their ends.
All inputs are finite; a program needn't handle non-finite values. No bound on the sum of `land_mask` on one device may be relied on, other than what follows from the above.
Results may differ from the reference program's by a relative error of at most 0.00002.
Values sent between devices are 32-bit elements; how exact they have to be, the bound alone decides.
No kernel may reach another device: no remote copies, remote signals or barrier semaphores. Data moves between devices by JAX's collectives and lax.ppermute only.
A program may use at most 128 MiB of HBM per device.

```python
import math
import jax
import jax.numpy as jnp
from jax import lax

NZ = 32
NX = 1024
NY = 1024


def place_ends(values, stream_key, least, largest):
    shape = values.shape
    place = [jax.random.randint(jax.random.fold_in(stream_key, axis), (), 0, shape[axis]) for axis in range(len(shape))]
    values = values.at[tuple(place)].set(least)
    longest = shape.index(max(shape))
    place[longest] = (place[longest] + 1) % shape[longest]
    return values.at[tuple(place)].set(largest)


def block_levels(stream_key, extent, split, least, high):
    factor_of = 1.0
    for position, shards_of in split:
        steps = jax.random.uniform(jax.random.fold_in(jax.random.fold_in(stream_key, 6), position), (shards_of,), jnp.float32, least / len(split), high / len(split))
        factor_of = factor_of * jnp.repeat(jnp.exp(steps), extent[position] // shards_of).reshape((-1,) + (1,) * (len(extent) - 1 - position))
    return factor_of


def centred(rng, dims, spread, most, pieces=(), dtype=jnp.bfloat16):
    drawn = spread * jax.random.normal(rng, dims, jnp.float32)
    if pieces:
        drawn = drawn * block_levels(rng, dims, pieces, -0.22, 0.18)
    return jnp.clip(drawn, -most, most).astype(dtype)


def setup_inputs(seed: int = 0) -> dict:
    splits = jax.random.split(jax.random.key(seed), 8)
    theta = jnp.clip(0.9 + 0.5 * jax.random.uniform(splits[0], (NZ, NX, NY), jnp.float32) ** block_levels(splits[0], (NZ, NX, NY), ((0, 8), (1, 4)), -0.2, 0.2), 0.9, 1.4)
    pressure = jnp.clip(jnp.exp(math.log(1.0) - 2.3025851 * jax.random.uniform(splits[1], (NZ, NX, NY), jnp.float32) ** block_levels(splits[1], (NZ, NX, NY), ((0, 8), (1, 4)), -0.2, 0.2)), 0.1, 1.0)
    vertical_wind = centred(splits[2], (NZ, NX, NY), 1.0, 6.0, ((0, 8), (1, 4)), jnp.float32)
    terrain = jnp.clip(0.5 * jax.random.uniform(splits[3], (NX, NY), jnp.float32) ** block_levels(splits[3], (NX, NY), ((0, 8), (1, 4)), -0.2, 0.2), 0.0, 0.5)
    column_mass = jnp.clip(0.5 + 0.5 * jax.random.uniform(splits[4], (NX, NY), jnp.float32) ** block_levels(splits[4], (NX, NY), ((0, 8), (1, 4)), -0.2, 0.2), 0.5, 1.0)
    land_mask = place_ends((jax.random.randint(splits[5], (NX, NY), 0, 2) < 1).astype(jnp.int32), jax.random.fold_in(splits[5], 1), 0, 1)
    pbl_top = place_ends(jax.random.randint(splits[6], (NX, NY), 2, NZ - 4), jax.random.fold_in(splits[6], 1), 2, (NZ - 4) - 1).astype(jnp.int32)
    return dict(theta=theta, pressure=pressure, vertical_wind=vertical_wind, terrain=terrain, column_mass=column_mass, land_mask=land_mask, pbl_top=pbl_top)


gamma_ratio = 1.4
smooth_rate = 0.2
lift_rate = 0.3
couple_rate = 0.5
land_boost = 0.5


def states(theta, pressure):
    alpha = theta * jnp.exp(-jnp.log(pressure) / gamma_ratio)
    sound_sq = gamma_ratio * pressure * alpha
    return alpha, sound_sq


def heights(terrain, column_mass, rising):
    return terrain[None] + column_mass[None] * rising / rising.shape[0]


def laplacian(padded):
    middle = padded[..., 1:-1, 1:-1]
    return padded[..., 2:, 1:-1] + padded[..., :-2, 1:-1] + padded[..., 1:-1, 2:] + padded[..., 1:-1, :-2] - 4.0 * middle


def column_solve(forcing, sound_sq, land_mask, pbl_top):
    levels = lax.broadcasted_iota(jnp.int32, forcing.shape, 0)
    inside = (land_mask[None] > 0) & (levels < pbl_top[None])
    damping = jnp.where(inside, 1.0 + land_boost, 1.0).astype(jnp.float32)
    couple = couple_rate * 0.5 * (sound_sq[:-1] + sound_sq[1:])
    zero_level = jnp.zeros_like(forcing[:1])
    below = jnp.concatenate([zero_level, couple], 0)
    above = jnp.concatenate([couple, zero_level], 0)
    centre = damping + below + above
    count = forcing.shape[0]
    ratios = []
    values = []
    ratio = above[0] / centre[0]
    value = forcing[0] / centre[0]
    ratios.append(ratio)
    values.append(value)
    for level in range(1, count):
        denom = centre[level] - below[level] * ratio
        value = (forcing[level] + below[level] * value) / denom
        ratio = above[level] / denom
        ratios.append(ratio)
        values.append(value)
    result = [None] * count
    current = values[count - 1]
    result[count - 1] = current
    for level in range(count - 2, -1, -1):
        current = values[level] + ratios[level] * current
        result[level] = current
    return jnp.stack(result, 0)


def reference(theta, pressure, vertical_wind, terrain, column_mass, land_mask, pbl_top):
    alpha, sound_sq = states(theta, pressure)
    rising = jnp.cumsum(alpha, axis=0)
    geopotential = heights(terrain, column_mass, rising)
    edges = ((0, 0), (1, 1), (1, 1))
    wind_pad = jnp.pad(vertical_wind, edges)
    geo_pad = jnp.pad(geopotential, edges)
    forcing = vertical_wind + smooth_rate * laplacian(wind_pad) + lift_rate * laplacian(geo_pad)
    updated_wind = column_solve(forcing, sound_sq, land_mask, pbl_top)
    return updated_wind, geopotential
```

```python
import jax
import jax.numpy as jnp
from jax import lax
from jax.experimental import pallas as pl
from jax.experimental.pallas import tpu as pltpu
from jax.sharding import PartitionSpec as P


gamma_ratio = 1.4
smooth_rate = 0.2
lift_rate = 0.3
couple_rate = 0.5
land_boost = 0.5


AXES = ("gx", "gy")
ANY = pl.BlockSpec(memory_space=pl.ANY)
SMEM = pl.BlockSpec(memory_space=pltpu.SMEM)
f32 = jnp.float32


def sds(*shape):
    return jax.ShapeDtypeStruct(shape, f32)


def states(theta, pressure):
    alpha = theta * jnp.exp(-jnp.log(pressure) / gamma_ratio)
    return alpha, gamma_ratio * pressure * alpha


def cost(nbytes, flops=0):
    return pl.CostEstimate(flops=flops, bytes_accessed=nbytes, transcendentals=0)


def split_slab(me, parts, after, H, C):
    arrays, steps, N = [], [], 0
    for members, (lv0, lv1), (r0, r1) in parts:
        for a in members:
            if not any(a is seen for seen in arrays):
                arrays.append(a)
            t = [a is seen for seen in arrays].index(True)
            for lv in range(lv0, lv1):
                steps.append((t, lv, r0, r1 - r0, N))
                N += r1 - r0
    nb = arrays[0].shape[1]

    def kernel(me_ref, *refs):
        ins = refs[: len(arrays)]
        outs = refs[len(arrays) + len(after) :][:H]
        stage, sem_in, sem_out = refs[len(arrays) + len(after) + H :]
        core, own = lax.rem(me_ref[0], nb), me_ref[1]
        loads = []
        for n, (t, lv, r0, rows, off) in enumerate(steps):
            loads.append(
                pltpu.make_async_copy(
                    ins[t].at[lv, core, pl.ds(r0, rows), :], stage.at[pl.ds(off, rows), :], sem_in.at[n]
                )
            )
            loads[-1].start()
        stores = []
        for n, (t, lv, r0, rows, off) in enumerate(steps):
            loads[n].wait()
            for m in [*range(1, H), 0]:
                block = lax.bitwise_xor(own, m)
                cols = pl.ds(pl.multiple_of(block * C, C), C)
                stores.append(
                    pltpu.make_async_copy(
                        stage.at[pl.ds(off, rows), cols], outs[m].at[pl.ds(off, rows), :], sem_out.at[n, m]
                    )
                )
                stores[-1].start()
        for c in stores:
            c.wait()

    return pl.pallas_call(
        kernel,
        out_shape=[sds(N, C)] * H,
        in_specs=[SMEM] + [ANY] * (len(arrays) + len(after)),
        out_specs=[ANY] * H,
        scratch_shapes=[
            pltpu.VMEM((N, H * C), f32),
            pltpu.SemaphoreType.DMA((len(steps),)),
            pltpu.SemaphoreType.DMA((len(steps), H)),
        ],
        cost_estimate=cost(8 * N * H * C),
    )(me, *arrays, *after)


def regroup(me, pieces, after, H, nb):
    N, C = pieces[0].shape

    def kernel(me_ref, *refs):
        ins, outs = refs[:H], refs[H + len(after) :][:H]
        stage, sem_in, sem_out = refs[H + len(after) + H :]
        z, j = lax.div(me_ref[0], nb), me_ref[1]
        loads = [
            pltpu.make_async_copy(ins[m], stage.at[lax.bitwise_xor(j, m)], sem_in.at[m]) for m in range(H)
        ]
        for c in loads:
            c.start()
        for c in loads:
            c.wait()
        stores = [
            pltpu.make_async_copy(stage.at[lax.bitwise_xor(z, q)], outs[q], sem_out.at[q])
            for q in far_first(H) + [0]
        ]
        for c in stores:
            c.start()
        for c in stores:
            c.wait()

    return pl.pallas_call(
        kernel,
        out_shape=[sds(N, C)] * H,
        in_specs=[SMEM] + [ANY] * (H + len(after)),
        out_specs=[ANY] * H,
        scratch_shapes=[
            pltpu.VMEM((H, N, C), f32),
            pltpu.SemaphoreType.DMA((H,)),
            pltpu.SemaphoreType.DMA((H,)),
        ],
        cost_estimate=cost(8 * H * N * C),
    )(me, *pieces, *after)


def far_first(H):
    return sorted(range(1, H), key=lambda q: (-q.bit_length(), q))


def moved(x, G, H, ds, dr):
    pairs = [(s * H + r, (s ^ ds) * H + (r ^ dr)) for s in range(G) for r in range(H)]
    return lax.ppermute(x, AXES, pairs)


def coefficients(me, chunks, layout, planes, rims, after, G, H, L, R, C):
    nz = G * L
    wide = -(-nz // 128) * 128
    flat = [p for chunk in chunks for p in chunk]

    def kernel(me_ref, terrain, mass, land, top, rim_t, rim_m, *refs):
        ins = refs[: len(flat)]
        geo, couple, inv, rim, west, east, th, pr, ra, sem = refs[len(flat) + len(after) :]
        i = me_ref[0]
        copies = []
        for c, parts in enumerate(layout):
            for q in range(H):
                src = ins[c * H + q]
                for what, e, lv0, levels, off in parts:
                    s = lax.bitwise_xor(i, q * (G // H) + e)
                    for lv in range(levels):
                        if what == 2:
                            rows, dst = ra.shape[1], ra.at[s]
                        else:
                            rows, dst = R, (th, pr)[what].at[s * L + lv0 + lv]
                        copies.append(
                            pltpu.make_async_copy(
                                src.at[pl.ds(off + lv * R, rows), :], dst, sem.at[len(copies)]
                            )
                        )
                        copies[-1].start()
        for c in copies:
            c.wait()

        run = jnp.zeros((2, C), f32)
        for s in range(G):
            for lv in range(L):
                run = run + ra[s, 2 * lv : 2 * lv + 2, :]
                rim[s * L + lv] = rim_t[...] + rim_m[...] * run / nz

        def rows_step(b, _):
            rows = pl.ds(pl.multiple_of(b * 8, 8), 8)
            ter, mas = terrain[rows, :], mass[rows, :]
            limit = jnp.where(land[rows, :] > 0, top[rows, :], 0)
            alpha, sound = states(th[0, rows, :], pr[0, rows, :])
            run = alpha
            below = jnp.zeros_like(alpha)
            ratio = jnp.zeros_like(alpha)
            lane = lax.broadcasted_iota(jnp.int32, (8, wide), 1)
            first = jnp.zeros((8, wide), f32)
            final = jnp.zeros((8, wide), f32)
            for k in range(nz):
                height = ter + mas * run / nz
                geo[k, rows, :] = height
                first = jnp.where(lane == k, height[:, :1], first)
                final = jnp.where(lane == k, height[:, C - 1 :], final)
                damping = jnp.where(k < limit, 1.0 + land_boost, 1.0).astype(f32)
                if k + 1 < nz:
                    alpha, sound_next = states(th[k + 1, rows, :], pr[k + 1, rows, :])
                    run = run + alpha
                    above = couple_rate * 0.5 * (sound + sound_next)
                    sound = sound_next
                else:
                    above = jnp.zeros_like(below)
                denom = damping + below + above - below * ratio
                rec = 1.0 / denom
                ratio = above * rec
                couple[k, rows, :] = above
                inv[k, rows, :] = rec
                below = above
            west[rows, :] = first
            east[rows, :] = final
            return 0

        lax.fori_loop(0, R // 8, rows_step, 0)

    VM = pl.BlockSpec(memory_space=pltpu.VMEM)
    ncopy = sum(levels for parts in layout for _, _, _, levels, _ in parts) * H
    return pl.pallas_call(
        kernel,
        out_shape=[sds(nz, R, C)] * 3 + [sds(nz, 2, C)] + [sds(R, wide)] * 2,
        in_specs=[SMEM] + [VM] * 6 + [ANY] * (len(flat) + len(after)),
        out_specs=[VM] * 6,
        scratch_shapes=[
            pltpu.VMEM((nz, R, C), f32),
            pltpu.VMEM((nz, R, C), f32),
            pltpu.VMEM((G, max(8, 2 * L), C), f32),
            pltpu.SemaphoreType.DMA((ncopy,)),
        ],
        cost_estimate=cost(24 * nz * R * C, 60 * nz * R * C),
    )(me, *planes, *rims, *flat, *after)


def lifted(me, geo, rim, west, east, after):
    nz, R, C = geo.shape
    deep = 4 if nz % 4 == 0 else 1

    def kernel(me_ref, geo_ref, rim_ref, west_ref, east_ref, *refs):
        out_ref = refs[-1]
        lane = lax.broadcasted_iota(jnp.int32, (R, C), 1)
        row = lax.broadcasted_iota(jnp.int32, (R, C), 0)
        level = lax.broadcasted_iota(jnp.int32, west_ref.shape, 1)
        for d in range(deep):
            here = level == pl.program_id(0) * deep + d
            column = lambda ref: jnp.sum(jnp.where(here, ref[...], 0.0), axis=1, keepdims=True)
            g = geo_ref[d]
            north = jnp.where(row == 0, rim_ref[d, 0:1, :], pltpu.roll(g, 1, 0))
            south = jnp.where(row == R - 1, rim_ref[d, 1:2, :], pltpu.roll(g, R - 1, 0))
            left = jnp.where(lane == 0, column(west_ref), pltpu.roll(g, 1, 1))
            right = jnp.where(lane == C - 1, column(east_ref), pltpu.roll(g, C - 1, 1))
            out_ref[d] = lift_rate * (south + north + right + left - 4.0 * g)

    block = lambda *shape: pl.BlockSpec((deep, *shape), lambda k: (k, 0, 0))
    side = pl.BlockSpec(west.shape, lambda k: (0, 0))
    return [
        pl.pallas_call(
            kernel,
            out_shape=sds(nz, R, C),
            grid=(nz // deep,),
            in_specs=[SMEM, block(R, C), block(2, C), side, side] + [ANY] * len(after),
            out_specs=block(R, C),
            cost_estimate=cost(8 * nz * R * C, 8 * nz * R * C),
        )(me, geo, rim, west, east, *after)
    ]


def smoothed(me, wind, before, behind, after):
    L, RS, Y = wind.shape

    def kernel(me_ref, wind_ref, before_ref, behind_ref, *refs):
        out_ref = refs[-1]
        lane = lax.broadcasted_iota(jnp.int32, (RS, Y), 1)
        row = lax.broadcasted_iota(jnp.int32, (RS, Y), 0)
        w = wind_ref[0]
        north = jnp.where(row == 0, before_ref[0], pltpu.roll(w, 1, 0))
        south = jnp.where(row == RS - 1, behind_ref[0], pltpu.roll(w, RS - 1, 0))
        left = jnp.where(lane == 0, 0.0, pltpu.roll(w, 1, 1))
        right = jnp.where(lane == Y - 1, 0.0, pltpu.roll(w, Y - 1, 1))
        out_ref[0] = w + smooth_rate * (south + north + right + left - 4.0 * w)

    block = lambda rows: pl.BlockSpec((1, rows, Y), lambda k: (k, 0, 0))
    return [
        pl.pallas_call(
            kernel,
            out_shape=sds(L, RS, Y),
            grid=(L,),
            in_specs=[SMEM, block(RS), block(1), block(1)] + [ANY] * len(after),
            out_specs=block(RS),
            cost_estimate=cost(8 * L * RS * Y, 8 * L * RS * Y),
        )(me, wind, before, behind, *after)
    ]


def substitute(me, pieces, lift, couple, inv, wind, r0, rows, G, H, L, R, C):
    nz = G * L
    nb = G // H
    held = [] if wind is None else [wind]

    def kernel(me_ref, lift_ref, couple_ref, inv_ref, *refs):
        ins = refs[:H]
        out, fo, li, co, iv, sem = refs[H + len(held) :]
        i = me_ref[0]
        where = pl.ds(r0, rows)
        copies = [
            pltpu.make_async_copy(lift_ref.at[:, where, :], li, sem.at[G]),
            pltpu.make_async_copy(couple_ref.at[:, where, :], co, sem.at[G + 1]),
            pltpu.make_async_copy(inv_ref.at[:, where, :], iv, sem.at[G + 2]),
        ]
        for k in range(G):
            s = lax.bitwise_xor(i, k)
            copies.append(
                pltpu.make_async_copy(
                    ins[k // nb].at[pl.ds(k % nb * (L * rows), L * rows), :],
                    fo.at[pl.ds(pl.multiple_of(s * (L * rows), 8), L * rows), :],
                    sem.at[k],
                )
            )
        for c in copies:
            c.start()
        for c in copies:
            c.wait()

        def step(b, _):
            base = pl.multiple_of(b * 8, 8)
            part = pl.ds(base, 8)
            value = jnp.zeros((8, C), f32)
            for k in range(nz):
                force = fo[pl.ds(pl.multiple_of(k * rows + base, 8), 8), :] + li[k, part, :]
                if k:
                    force = force + co[k - 1, part, :] * value
                value = force * iv[k, part, :]
                li[k, part, :] = value
            for k in range(nz - 2, -1, -1):
                value = li[k, part, :] + (co[k, part, :] * iv[k, part, :]) * value
                li[k, part, :] = value
            return 0

        lax.fori_loop(0, rows // 8, step, 0)
        done = pltpu.make_async_copy(li, out.at[:, where, :], sem.at[G + 3])
        done.start()
        done.wait()

    return pl.pallas_call(
        kernel,
        out_shape=sds(nz, R, C),
        in_specs=[SMEM] + [ANY] * (3 + H + len(held)),
        out_specs=ANY,
        scratch_shapes=[
            pltpu.VMEM((nz * rows, C), f32),
            pltpu.VMEM((nz, rows, C), f32),
            pltpu.VMEM((nz, rows, C), f32),
            pltpu.VMEM((nz, rows, C), f32),
            pltpu.SemaphoreType.DMA((G + 4,)),
        ],
        input_output_aliases={4 + H: 0} if held else {},
        cost_estimate=cost(20 * nz * rows * C, 8 * nz * rows * C),
    )(me, lift, couple, inv, *pieces, *held)


def on_device(theta, pressure, vertical_wind, terrain, column_mass, land_mask, pbl_top):
    G, H = lax.axis_size("gx"), lax.axis_size("gy")
    nb = G // H
    L, RS, Y = theta.shape
    R, C = RS // nb, Y // H
    s, r = lax.axis_index("gx"), lax.axis_index("gy")
    me = jnp.stack([s, r]).astype(jnp.int32)
    slab = lambda a: a.reshape(a.shape[0], nb, -1, Y)
    after = []

    def step(kernel, *args):
        out = kernel(me, *args)
        after[:] = [out[0]]
        return out

    def send_to(x, ds, dr):
        return moved(x, G, H, ds, dr)

    def beside(x, axis, up):
        n = lax.axis_size(axis)
        pairs = [(i, i + 1) if up else (i + 1, i) for i in range(n - 1)]
        return lax.ppermute(x, axis, pairs)

    def family(a):
        return [slab(a)] + [slab(send_to(a, e, 0)) for e in range(1, nb)]

    def cut(parts):
        pieces = step(split_slab, parts, list(after), H, C)
        return [pieces[0]] + [send_to(pieces[m], 0, m) for m in range(1, H)]

    def send(pieces, behind_of=()):
        pieces = step(regroup, pieces, [*after, *behind_of], H, nb)
        out = [pieces[0]] + [None] * (H - 1)
        for q in far_first(H):
            out[q] = send_to(pieces[q], q * nb, 0)
        return out

    def later(*x):
        return lax.optimization_barrier((*x, *after))[: len(x)]

    full = (0, R)
    first = cut([(family(theta[:1]), (0, 1), full)])

    th = family(later(theta)[0])
    mid_levels = max(1, min(3, L - 1))
    second = cut([(th, (1, mid_levels), full)]) if mid_levels > 1 else None
    sources = later(pressure)
    pr = family(sources[0])
    lead = [send(first)]
    layout = [[(0, e, 0, 1, e * R) for e in range(nb)]]

    half = max(1, L // 2)
    third = cut([(th, (mid_levels, L), full), (pr, (0, half), full)])

    sources = later(theta, pressure, vertical_wind)
    before = beside(jnp.stack([a[:, RS - 1 :] for a in sources]), "gy", True)
    behind = beside(jnp.stack([a[:, :1] for a in sources]), "gy", False)

    if second is not None:
        lead.append(send(second))
        n = mid_levels - 1
        layout.append([(0, e, 1, n, e * n * R) for e in range(nb)])

    blown = step(smoothed, vertical_wind, before[2], behind[2], list(after))[0]
    safe = lambda p: jnp.where(p > 0, p, 1.0)
    theta, pressure, before, behind = later(theta, pressure, before, behind)
    rims = []
    for b in range(nb):
        lines = []
        for lo, src in ((b * R - 1, before), ((b + 1) * R, behind)):
            if 0 <= lo < RS:
                t, p = theta[:, lo, :], pressure[:, lo, :]
            else:
                t, p = src[0, :, 0, :], safe(src[1, :, 0, :])
            lines.append(states(t, p)[0])
        rims.append(jnp.stack(lines, 1).reshape(2 * L, Y))
    tall = -(-2 * L // 8) * 8
    rim = jnp.pad(jnp.stack(rims), ((0, 0), (0, tall - 2 * L), (0, 0))).reshape(1, nb * tall, Y)
    rim, blown = family(rim), family(blown)

    fourth = cut([(pr, (half, L), full), (rim, (0, 1), (0, tall))])
    lead.append(send(third))
    plane_rim = lambda a: jnp.concatenate([beside(a[-1:], "gx", True), beside(a[:1], "gx", False)], 0)
    rim_planes = [plane_rim(a) for a in later(terrain, column_mass)]
    n, base = L - mid_levels, nb * (L - mid_levels) * R
    layout.append(
        [(0, e, mid_levels, n, e * n * R) for e in range(nb)]
        + [(1, e, 0, half, base + e * half * R) for e in range(nb)]
    )
    last = max(8, R // 4 // 8 * 8)
    rows_cut = [(0, R - last), (R - last, R)]
    cuts = [cut([(blown, (0, L), rows_cut[0])])]
    lead.append(send(fourth))
    n = L - half
    layout.append(
        [(1, e, half, n, e * n * R) for e in range(nb)]
        + [(2, e, 0, 1, nb * n * R + e * tall) for e in range(nb)]
    )
    cuts.append(cut([(blown, (0, L), rows_cut[1])]))
    winds = [send(cuts[0], lead[-2][1:])]

    planes = (terrain, column_mass, land_mask, pbl_top)
    geo, couple, inv, rim_geo, west, east = step(
        coefficients, lead, layout, planes, rim_planes, list(after), G, H, L, R, C
    )
    west, east = beside(east, "gy", True), beside(west, "gy", False)
    lift = step(lifted, geo, rim_geo, west, east, list(after))[0]
    winds.append(send(cuts[1]))

    wind = None
    for (r0, r1), pieces in zip(rows_cut, winds):
        wind = substitute(me, pieces, lift, couple, inv, wind, r0, r1 - r0, G, H, L, R, C)
    return wind, geo


def solution(mesh):
    placed = (P("gx", "gy", None),) * 3 + (P("gx", "gy"),) * 4

    fn = jax.shard_map(
        on_device,
        mesh=mesh,
        in_specs=placed,
        out_specs=(P(None, "gx", "gy"), P(None, "gx", "gy")),
        check_vma=False,
    )

    def traced(*args):
        jax.eval_shape(fn, *args)
        return fn(*args)

    return traced
```

```python
import jax
import jax.numpy as jnp
from jax import lax
from jax.experimental import pallas as pl
from jax.experimental.pallas import tpu as pltpu
from jax.sharding import PartitionSpec as P


gamma_ratio = 1.4
smooth_rate = 0.2
lift_rate = 0.3
couple_rate = 0.5
land_boost = 0.5


AXES = ("gx", "gy")
ANY = pl.BlockSpec(memory_space=pl.ANY)
f32 = jnp.float32
WHOLE = pltpu.CompilerParams(vmem_limit_bytes=67043328)


def sds(*shape):
    return jax.ShapeDtypeStruct(shape, f32)


def states(theta, pressure):
    alpha = theta * jnp.exp(-jnp.log(pressure) / gamma_ratio)
    return alpha, gamma_ratio * pressure * alpha


def cost(nbytes, flops=0):
    return pl.CostEstimate(flops=flops, bytes_accessed=nbytes, transcendentals=0)


def split_slab(parts, after, H, C, far=1):
    arrays, steps, N = [], [], 0
    for members, (lv0, lv1), (r0, r1) in parts:
        for a in members:
            if not any(a is seen for seen in arrays):
                arrays.append(a)
            t = [a is seen for seen in arrays].index(True)
            for lv in range(lv0, lv1):
                steps.append((t, lv, r0, r1 - r0, N))
                N += r1 - r0
    nb = arrays[0].shape[1]
    work = [(e, one) for e in range(far) for one in steps]

    def kernel(*refs):
        ins = refs[: len(arrays)]
        outs = refs[len(arrays) + len(after) :][: far * H]
        stage, sem_in, sem_out = refs[len(arrays) + len(after) + far * H :]
        core, own = lax.rem(lax.axis_index("gx"), nb), lax.axis_index("gy")
        loads = []
        for n, (e, (t, lv, r0, rows, off)) in enumerate(work):
            loads.append(
                pltpu.make_async_copy(
                    ins[t].at[lv, lax.bitwise_xor(core, e), pl.ds(r0, rows), :],
                    stage.at[e, pl.ds(off, rows), :],
                    sem_in.at[n],
                )
            )
            loads[-1].start()
        stores = []
        for n, (e, (t, lv, r0, rows, off)) in enumerate(work):
            loads[n].wait()
            for m in [*range(1, H), 0]:
                block = lax.bitwise_xor(own, m)
                cols = pl.ds(pl.multiple_of(block * C, C), C)
                stores.append(
                    pltpu.make_async_copy(
                        stage.at[e, pl.ds(off, rows), cols],
                        outs[e * H + m].at[pl.ds(off, rows), :],
                        sem_out.at[n, m],
                    )
                )
                stores[-1].start()
        for c in stores:
            c.wait()

    return pl.pallas_call(
        kernel,
        out_shape=[sds(N, C)] * (far * H),
        in_specs=[ANY] * (len(arrays) + len(after)),
        out_specs=[ANY] * (far * H),
        scratch_shapes=[
            pltpu.VMEM((far, N, H * C), f32),
            pltpu.SemaphoreType.DMA((len(work),)),
            pltpu.SemaphoreType.DMA((len(work), H)),
        ],
        compiler_params=WHOLE,
        cost_estimate=cost(8 * far * N * H * C),
    )(*arrays, *after)


def regroup(pieces, after, H, nb):
    C = pieces[0][0].shape[1]
    rows = [group[0].shape[0] for group in pieces]
    N = sum(rows)
    flat = [p for group in pieces for p in group]

    def kernel(*refs):
        ins, outs = refs[: len(flat)], refs[len(flat) + len(after) :][:H]
        stage, sem_in, sem_out = refs[len(flat) + len(after) + H :]
        z, j = lax.div(lax.axis_index("gx"), nb), lax.axis_index("gy")
        loads = [
            pltpu.make_async_copy(
                ins[g * H + m],
                stage.at[lax.bitwise_xor(j, m), pl.ds(sum(rows[:g]), rows[g]), :],
                sem_in.at[g * H + m],
            )
            for g in range(len(rows))
            for m in range(H)
        ]
        for c in loads:
            c.start()
        for c in loads:
            c.wait()
        stores = [
            pltpu.make_async_copy(stage.at[lax.bitwise_xor(z, q)], outs[q], sem_out.at[q])
            for q in partners(H) + [0]
        ]
        for c in stores:
            c.start()
        for c in stores:
            c.wait()

    return pl.pallas_call(
        kernel,
        out_shape=[sds(N, C)] * H,
        in_specs=[ANY] * (len(flat) + len(after)),
        out_specs=[ANY] * H,
        scratch_shapes=[
            pltpu.VMEM((H, N, C), f32),
            pltpu.SemaphoreType.DMA((len(flat),)),
            pltpu.SemaphoreType.DMA((H,)),
        ],
        compiler_params=WHOLE,
        cost_estimate=cost(8 * H * N * C),
    )(*flat, *after)


def partners(H):
    return list(range(1, H))


def moved(x, G, H, ds, dr):
    pairs = [(s * H + r, (s ^ ds) * H + (r ^ dr)) for s in range(G) for r in range(H)]
    return lax.ppermute(x, AXES, pairs)


def coefficients(chunks, layout, planes, rims, after, G, H, L, R, C):
    nz = G * L
    wide = -(-nz // 128) * 128
    flat = [p for chunk in chunks for p in chunk]

    def kernel(terrain, mass, land, top, rim_t, rim_m, *refs):
        ins = refs[: len(flat)]
        geo, couple, inv, rim, west, east, th, pr, ra, sem = refs[len(flat) + len(after) :]
        i = lax.axis_index("gx")
        copies = []
        for c, parts in enumerate(layout):
            for q in range(H):
                src = ins[c * H + q]
                for what, e, lv0, levels, off in parts:
                    s = lax.bitwise_xor(i, q * (G // H) + e)
                    for lv in range(levels):
                        if what == 2:
                            rows, dst = ra.shape[1], ra.at[s]
                        else:
                            rows, dst = R, (th, pr)[what].at[s * L + lv0 + lv]
                        copies.append(
                            pltpu.make_async_copy(
                                src.at[pl.ds(off + lv * R, rows), :], dst, sem.at[len(copies)]
                            )
                        )
                        copies[-1].start()
        for c in copies:
            c.wait()

        run = jnp.zeros((2, C), f32)
        for s in range(G):
            for lv in range(L):
                run = run + ra[s, 2 * lv : 2 * lv + 2, :]
                rim[s * L + lv] = rim_t[...] + rim_m[...] * run / nz

        def rows_step(b, _):
            rows = pl.ds(pl.multiple_of(b * 8, 8), 8)
            ter, mas = terrain[rows, :], mass[rows, :]
            limit = jnp.where(land[rows, :] > 0, top[rows, :], 0)
            alpha, sound = states(th[0, rows, :], pr[0, rows, :])
            run = alpha
            below = jnp.zeros_like(alpha)
            ratio = jnp.zeros_like(alpha)
            lane = lax.broadcasted_iota(jnp.int32, (8, wide), 1)
            first = jnp.zeros((8, wide), f32)
            final = jnp.zeros((8, wide), f32)
            for k in range(nz):
                height = ter + mas * run / nz
                geo[k, rows, :] = height
                first = jnp.where(lane == k, height[:, :1], first)
                final = jnp.where(lane == k, height[:, C - 1 :], final)
                damping = jnp.where(k < limit, 1.0 + land_boost, 1.0).astype(f32)
                if k + 1 < nz:
                    alpha, sound_next = states(th[k + 1, rows, :], pr[k + 1, rows, :])
                    run = run + alpha
                    above = couple_rate * 0.5 * (sound + sound_next)
                    sound = sound_next
                else:
                    above = jnp.zeros_like(below)
                denom = damping + below + above - below * ratio
                rec = 1.0 / denom
                ratio = above * rec
                couple[k, rows, :] = above
                inv[k, rows, :] = rec
                below = above
            west[rows, :] = first
            east[rows, :] = final
            return 0

        lax.fori_loop(0, R // 8, rows_step, 0)

    VM = pl.BlockSpec(memory_space=pltpu.VMEM)
    ncopy = sum(levels for parts in layout for _, _, _, levels, _ in parts) * H
    return pl.pallas_call(
        kernel,
        out_shape=[sds(nz, R, C)] * 3 + [sds(nz, 2, C)] + [sds(R, wide)] * 2,
        in_specs=[VM] * 6 + [ANY] * (len(flat) + len(after)),
        out_specs=[VM] * 6,
        scratch_shapes=[
            pltpu.VMEM((nz, R, C), f32),
            pltpu.VMEM((nz, R, C), f32),
            pltpu.VMEM((G, max(8, 2 * L), C), f32),
            pltpu.SemaphoreType.DMA((ncopy,)),
        ],
        cost_estimate=cost(24 * nz * R * C, 60 * nz * R * C),
    )(*planes, *rims, *flat, *after)


def lifted(geo, rim, west, east, after):
    nz, R, C = geo.shape
    deep = 4 if nz % 4 == 0 else 1

    def kernel(geo_ref, rim_ref, west_ref, east_ref, *refs):
        out_ref = refs[-1]
        lane = lax.broadcasted_iota(jnp.int32, (R, C), 1)
        row = lax.broadcasted_iota(jnp.int32, (R, C), 0)
        level = lax.broadcasted_iota(jnp.int32, west_ref.shape, 1)
        for d in range(deep):
            here = level == pl.program_id(0) * deep + d
            column = lambda ref: jnp.sum(jnp.where(here, ref[...], 0.0), axis=1, keepdims=True)
            g = geo_ref[d]
            north = jnp.where(row == 0, rim_ref[d, 0:1, :], pltpu.roll(g, 1, 0))
            south = jnp.where(row == R - 1, rim_ref[d, 1:2, :], pltpu.roll(g, R - 1, 0))
            left = jnp.where(lane == 0, column(west_ref), pltpu.roll(g, 1, 1))
            right = jnp.where(lane == C - 1, column(east_ref), pltpu.roll(g, C - 1, 1))
            out_ref[d] = lift_rate * (south + north + right + left - 4.0 * g)

    block = lambda *shape: pl.BlockSpec((deep, *shape), lambda k: (k, 0, 0))
    side = pl.BlockSpec(west.shape, lambda k: (0, 0))
    return [
        pl.pallas_call(
            kernel,
            out_shape=sds(nz, R, C),
            grid=(nz // deep,),
            in_specs=[block(R, C), block(2, C), side, side] + [ANY] * len(after),
            out_specs=block(R, C),
            cost_estimate=cost(8 * nz * R * C, 8 * nz * R * C),
        )(geo, rim, west, east, *after)
    ]


def smoothed(wind, before, behind, after):
    L, RS, Y = wind.shape

    def kernel(wind_ref, before_ref, behind_ref, *refs):
        out_ref = refs[-1]
        lane = lax.broadcasted_iota(jnp.int32, (RS, Y), 1)
        row = lax.broadcasted_iota(jnp.int32, (RS, Y), 0)
        w = wind_ref[0]
        north = jnp.where(row == 0, before_ref[0], pltpu.roll(w, 1, 0))
        south = jnp.where(row == RS - 1, behind_ref[0], pltpu.roll(w, RS - 1, 0))
        left = jnp.where(lane == 0, 0.0, pltpu.roll(w, 1, 1))
        right = jnp.where(lane == Y - 1, 0.0, pltpu.roll(w, Y - 1, 1))
        out_ref[0] = w + smooth_rate * (south + north + right + left - 4.0 * w)

    block = lambda rows: pl.BlockSpec((1, rows, Y), lambda k: (k, 0, 0))
    return [
        pl.pallas_call(
            kernel,
            out_shape=sds(L, RS, Y),
            grid=(L,),
            in_specs=[block(RS), block(1), block(1)] + [ANY] * len(after),
            out_specs=block(RS),
            cost_estimate=cost(8 * L * RS * Y, 8 * L * RS * Y),
        )(wind, before, behind, *after)
    ]


def substitute(pieces, lift, couple, inv, wind, r0, rows, G, H, L, R, C):
    nz = G * L
    nb = G // H
    tall = 8
    held = [] if wind is None else [wind]
    pieces = [p.reshape(nb * L, rows, C) for p in pieces]

    def kernel(lift_ref, couple_ref, inv_ref, *refs):
        ins = refs[:H]
        out, fo, li, co, iv, sem, sem_out = refs[H + len(held) :]
        i = lax.axis_index("gx")

        def loads(b):
            part = pl.ds(pl.multiple_of(b * tall, tall), tall)
            where = pl.ds(pl.multiple_of(r0 + b * tall, tall), tall)
            copies = []
            for src, dst in ((lift_ref, li), (couple_ref, co), (inv_ref, iv)):
                copies.append(
                    pltpu.make_async_copy(src.at[:, where, :], dst.at[:, part, :], sem.at[b, len(copies)])
                )
            for k in range(G):
                s = lax.bitwise_xor(i, k)
                copies.append(
                    pltpu.make_async_copy(
                        ins[k // nb].at[pl.ds(k % nb * L, L), part, :],
                        fo.at[pl.ds(s * L, L), part, :],
                        sem.at[b, len(copies)],
                    )
                )
            return copies

        def store(b):
            part = pl.ds(pl.multiple_of(b * tall, tall), tall)
            where = pl.ds(pl.multiple_of(r0 + b * tall, tall), tall)
            return pltpu.make_async_copy(li.at[:, part, :], out.at[:, where, :], sem_out.at[b])

        def begin(b, _):
            for c in loads(b):
                c.start()
            return 0

        def sweep(b, _):
            for c in loads(b):
                c.wait()
            part = pl.ds(pl.multiple_of(b * tall, tall), tall)
            value = jnp.zeros((tall, C), f32)
            for k in range(nz):
                force = fo[k, part, :] + li[k, part, :]
                if k:
                    force = force + co[k - 1, part, :] * value
                value = force * iv[k, part, :]
                li[k, part, :] = value
            for k in range(nz - 2, -1, -1):
                value = li[k, part, :] + (co[k, part, :] * iv[k, part, :]) * value
                li[k, part, :] = value
            store(b).start()
            return 0

        def finish(b, _):
            store(b).wait()
            return 0

        for stage in (begin, sweep, finish):
            lax.fori_loop(0, rows // tall, stage, 0)

    return pl.pallas_call(
        kernel,
        out_shape=sds(nz, R, C),
        in_specs=[ANY] * (3 + H + len(held)),
        out_specs=ANY,
        scratch_shapes=[pltpu.VMEM((nz, rows, C), f32)] * 4
        + [
            pltpu.SemaphoreType.DMA((rows // tall, G + 3)),
            pltpu.SemaphoreType.DMA((rows // tall,)),
        ],
        input_output_aliases={3 + H: 0} if held else {},
        compiler_params=WHOLE,
        cost_estimate=cost(20 * nz * rows * C, 8 * nz * rows * C),
    )(lift, couple, inv, *pieces, *held)


def on_device(theta, pressure, vertical_wind, terrain, column_mass, land_mask, pbl_top):
    G, H = lax.axis_size("gx"), lax.axis_size("gy")
    nb = G // H
    L, RS, Y = theta.shape
    R, C = RS // nb, Y // H
    slab = lambda a: a.reshape(a.shape[0], nb, -1, Y)
    after = []

    def step(kernel, *args):
        out = kernel(*args)
        after[:] = [out[0]]
        return out

    def send_to(x, ds, dr):
        return moved(x, G, H, ds, dr)

    def beside(x, axis, up):
        n = lax.axis_size(axis)
        pairs = [(i, i + 1) if up else (i + 1, i) for i in range(n - 1)]
        return lax.ppermute(x, axis, pairs)

    def family(a):
        return [slab(a)] + [slab(send_to(a, e, 0)) for e in range(1, nb)]

    def cut(parts, far=1):
        pieces = step(split_slab, parts, list(after), H, C, far)
        out = [pieces[0]] + [send_to(pieces[m], 0, m) for m in range(1, H)]
        for e in range(1, far):
            out += [send_to(pieces[e * H + m], e, m) for m in range(H)]
        return [out[e * H : e * H + H] for e in range(far)]

    def send(pieces, behind_of=()):
        pieces = step(regroup, pieces, [*after, *behind_of], H, nb)
        out = [pieces[0]] + [None] * (H - 1)
        for q in partners(H):
            out[q] = send_to(pieces[q], q * nb, 0)
        return out

    def later(*x):
        return lax.optimization_barrier((*x, *after))[: len(x)]

    full = (0, R)
    th = family(theta)
    first = cut([([slab(theta)], (0, 1), full)], nb)
    mid_levels = max(1, min(3, L - 1))
    second = cut([(th, (1, mid_levels), full)]) if mid_levels > 1 else None
    pr = family(later(pressure)[0])
    lead = [send(first)]
    layout = [[(0, e, 0, 1, e * R) for e in range(nb)]]

    half = max(1, L // 2)
    third = cut([(th, (mid_levels, L), full), (pr, (0, half), full)])

    sources = later(theta, pressure, vertical_wind)
    before = beside(jnp.stack([a[:, RS - 1 :] for a in sources]), "gy", True)
    behind = beside(jnp.stack([a[:, :1] for a in sources]), "gy", False)

    if second is not None:
        lead.append(send(second))
        n = mid_levels - 1
        layout.append([(0, e, 1, n, e * n * R) for e in range(nb)])
    lead.append(send(third))
    n, base = L - mid_levels, nb * (L - mid_levels) * R
    layout.append(
        [(0, e, mid_levels, n, e * n * R) for e in range(nb)]
        + [(1, e, 0, half, base + e * half * R) for e in range(nb)]
    )

    blown = step(smoothed, vertical_wind, before[2], behind[2], list(after))[0]
    safe = lambda p: jnp.where(p > 0, p, 1.0)
    theta, pressure, before, behind = later(theta, pressure, before, behind)
    rims = []
    for b in range(nb):
        lines = []
        for lo, src in ((b * R - 1, before), ((b + 1) * R, behind)):
            if 0 <= lo < RS:
                t, p = theta[:, lo, :], pressure[:, lo, :]
            else:
                t, p = src[0, :, 0, :], safe(src[1, :, 0, :])
            lines.append(states(t, p)[0])
        rims.append(jnp.stack(lines, 1).reshape(2 * L, Y))
    tall = -(-2 * L // 8) * 8
    rim = jnp.pad(jnp.stack(rims), ((0, 0), (0, tall - 2 * L), (0, 0))).reshape(1, nb * tall, Y)
    rim, blown = family(rim), family(blown)

    fourth = cut([(pr, (half, L), full), (rim, (0, 1), (0, tall))])
    part, last = max(8, R // 4 // 8 * 8), max(8, R // 4 // 8 * 8)
    marks = sorted({0, min(part, R), max(R - last, min(part, R)), R})
    rows_cut = list(zip(marks[:-1], marks[1:]))
    cuts = [cut([(blown, (0, L), rows_cut[0])])]
    lead.append(send(fourth))
    plane_rim = lambda a: jnp.concatenate([beside(a[-1:], "gx", True), beside(a[:1], "gx", False)], 0)
    rim_planes = [plane_rim(a) for a in later(terrain, column_mass)]
    n = L - half
    layout.append(
        [(1, e, half, n, e * n * R) for e in range(nb)]
        + [(2, e, 0, 1, nb * n * R + e * tall) for e in range(nb)]
    )
    cuts += [cut([(blown, (0, L), rows)]) for rows in rows_cut[1:]]
    winds = [send(cuts[0], lead[-2][1:])]
    winds += [send(pieces, lead[-1][1:]) for pieces in cuts[1:-1]]

    planes = (terrain, column_mass, land_mask, pbl_top)
    geo, couple, inv, rim_geo, west, east = step(
        coefficients, lead, layout, planes, rim_planes, list(after), G, H, L, R, C
    )
    west, east = beside(east, "gy", True), beside(west, "gy", False)
    winds += [send(pieces) for pieces in cuts[len(winds) :]]
    lift = step(lifted, geo, rim_geo, west, east, list(after))[0]

    wind = None
    for (r0, r1), pieces in zip(rows_cut, winds):
        wind = substitute(pieces, lift, couple, inv, wind, r0, r1 - r0, G, H, L, R, C)
    return wind, geo


def solution(mesh):
    placed = (P("gx", "gy", None),) * 3 + (P("gx", "gy"),) * 4

    fn = jax.shard_map(
        on_device,
        mesh=mesh,
        in_specs=placed,
        out_specs=(P(None, "gx", "gy"), P(None, "gx", "gy")),
        check_vma=False,
    )

    def traced(*args):
        jax.eval_shape(fn, *args)
        return fn(*args)

    return traced
```

```python
import jax
import jax.numpy as jnp
from jax import lax
from jax.experimental import pallas as pl
from jax.experimental.pallas import tpu as pltpu
from jax.sharding import PartitionSpec as P


gamma_ratio = 1.4
smooth_rate = 0.2
lift_rate = 0.3
couple_rate = 0.5
land_boost = 0.5


AXES = ("gx", "gy")
ANY = pl.BlockSpec(memory_space=pl.ANY)
f32 = jnp.float32
WHOLE = pltpu.CompilerParams(vmem_limit_bytes=67043328)


def sds(*shape):
    return jax.ShapeDtypeStruct(shape, f32)


def states(theta, pressure):
    alpha = theta * jnp.exp(-jnp.log(pressure) / gamma_ratio)
    return alpha, gamma_ratio * pressure * alpha


def cost(nbytes, flops=0):
    return pl.CostEstimate(flops=flops, bytes_accessed=nbytes, transcendentals=0)


def split_slab(parts, after, H, C, far=1):
    arrays, steps, N = [], [], 0
    for members, (lv0, lv1), (r0, r1) in parts:
        for a in members:
            if not any(a is seen for seen in arrays):
                arrays.append(a)
            t = [a is seen for seen in arrays].index(True)
            for lv in range(lv0, lv1):
                steps.append((t, lv, r0, r1 - r0, N))
                N += r1 - r0
    nb = arrays[0].shape[1]
    work = [(e, one) for e in range(far) for one in steps]

    def kernel(*refs):
        ins = refs[: len(arrays)]
        outs = refs[len(arrays) + len(after) :][: far * H]
        stage, sem_in, sem_out = refs[len(arrays) + len(after) + far * H :]
        core, own = lax.rem(lax.axis_index("gx"), nb), lax.axis_index("gy")
        loads = []
        for n, (e, (t, lv, r0, rows, off)) in enumerate(work):
            loads.append(
                pltpu.make_async_copy(
                    ins[t].at[lv, lax.bitwise_xor(core, e), pl.ds(r0, rows), :],
                    stage.at[e, pl.ds(off, rows), :],
                    sem_in.at[n],
                )
            )
            loads[-1].start()
        stores = []
        for n, (e, (t, lv, r0, rows, off)) in enumerate(work):
            loads[n].wait()
            for m in [*range(1, H), 0]:
                block = lax.bitwise_xor(own, m)
                cols = pl.ds(pl.multiple_of(block * C, C), C)
                stores.append(
                    pltpu.make_async_copy(
                        stage.at[e, pl.ds(off, rows), cols],
                        outs[e * H + m].at[pl.ds(off, rows), :],
                        sem_out.at[n, m],
                    )
                )
                stores[-1].start()
        for c in stores:
            c.wait()

    return pl.pallas_call(
        kernel,
        out_shape=[sds(N, C)] * (far * H),
        in_specs=[ANY] * (len(arrays) + len(after)),
        out_specs=[ANY] * (far * H),
        scratch_shapes=[
            pltpu.VMEM((far, N, H * C), f32),
            pltpu.SemaphoreType.DMA((len(work),)),
            pltpu.SemaphoreType.DMA((len(work), H)),
        ],
        compiler_params=WHOLE,
        cost_estimate=cost(8 * far * N * H * C),
    )(*arrays, *after)


def regroup(pieces, after, H, nb):
    C = pieces[0][0].shape[1]
    rows = [group[0].shape[0] for group in pieces]
    N = sum(rows)
    flat = [p for group in pieces for p in group]

    def kernel(*refs):
        ins, outs = refs[: len(flat)], refs[len(flat) + len(after) :][:H]
        stage, sem_in, sem_out = refs[len(flat) + len(after) + H :]
        z, j = lax.div(lax.axis_index("gx"), nb), lax.axis_index("gy")
        loads = [
            pltpu.make_async_copy(
                ins[g * H + m],
                stage.at[lax.bitwise_xor(j, m), pl.ds(sum(rows[:g]), rows[g]), :],
                sem_in.at[g * H + m],
            )
            for g in range(len(rows))
            for m in range(H)
        ]
        for c in loads:
            c.start()
        for c in loads:
            c.wait()
        stores = [
            pltpu.make_async_copy(stage.at[lax.bitwise_xor(z, q)], outs[q], sem_out.at[q])
            for q in partners(H) + [0]
        ]
        for c in stores:
            c.start()
        for c in stores:
            c.wait()

    return pl.pallas_call(
        kernel,
        out_shape=[sds(N, C)] * H,
        in_specs=[ANY] * (len(flat) + len(after)),
        out_specs=[ANY] * H,
        scratch_shapes=[
            pltpu.VMEM((H, N, C), f32),
            pltpu.SemaphoreType.DMA((len(flat),)),
            pltpu.SemaphoreType.DMA((H,)),
        ],
        compiler_params=WHOLE,
        cost_estimate=cost(8 * H * N * C),
    )(*flat, *after)


def partners(H):
    return list(range(1, H))


def moved(x, G, H, ds, dr):
    pairs = [(s * H + r, (s ^ ds) * H + (r ^ dr)) for s in range(G) for r in range(H)]
    return lax.ppermute(x, AXES, pairs)


def coefficients(chunks, layout, planes, rims, after, G, H, L, R, C):
    nz = G * L
    wide = -(-nz // 128) * 128
    flat = [p for chunk in chunks for p in chunk]

    def kernel(terrain, mass, land, top, rim_t, rim_m, *refs):
        ins = refs[: len(flat)]
        geo, couple, inv, rim, west, east, th, pr, ra, sem = refs[len(flat) + len(after) :]
        i = lax.axis_index("gx")
        copies = []
        for c, parts in enumerate(layout):
            for q in range(H):
                src = ins[c * H + q]
                for what, e, lv0, levels, off in parts:
                    s = lax.bitwise_xor(i, q * (G // H) + e)
                    for lv in range(levels):
                        if what == 2:
                            rows, dst = ra.shape[1], ra.at[s]
                        else:
                            rows, dst = R, (th, pr)[what].at[s * L + lv0 + lv]
                        copies.append(
                            pltpu.make_async_copy(
                                src.at[pl.ds(off + lv * R, rows), :], dst, sem.at[len(copies)]
                            )
                        )
                        copies[-1].start()
        for c in copies:
            c.wait()

        run = jnp.zeros((2, C), f32)
        for s in range(G):
            for lv in range(L):
                run = run + ra[s, 2 * lv : 2 * lv + 2, :]
                rim[s * L + lv] = rim_t[...] + rim_m[...] * run / nz

        def rows_step(b, _):
            rows = pl.ds(pl.multiple_of(b * 8, 8), 8)
            ter, mas = terrain[rows, :], mass[rows, :]
            limit = jnp.where(land[rows, :] > 0, top[rows, :], 0)
            alpha, sound = states(th[0, rows, :], pr[0, rows, :])
            run = alpha
            below = jnp.zeros_like(alpha)
            ratio = jnp.zeros_like(alpha)
            lane = lax.broadcasted_iota(jnp.int32, (8, wide), 1)
            first = jnp.zeros((8, wide), f32)
            final = jnp.zeros((8, wide), f32)
            for k in range(nz):
                height = ter + mas * run / nz
                geo[k, rows, :] = height
                first = jnp.where(lane == k, height[:, :1], first)
                final = jnp.where(lane == k, height[:, C - 1 :], final)
                damping = jnp.where(k < limit, 1.0 + land_boost, 1.0).astype(f32)
                if k + 1 < nz:
                    alpha, sound_next = states(th[k + 1, rows, :], pr[k + 1, rows, :])
                    run = run + alpha
                    above = couple_rate * 0.5 * (sound + sound_next)
                    sound = sound_next
                else:
                    above = jnp.zeros_like(below)
                denom = damping + below + above - below * ratio
                rec = 1.0 / denom
                ratio = above * rec
                couple[k, rows, :] = above
                inv[k, rows, :] = rec
                below = above
            west[rows, :] = first
            east[rows, :] = final
            return 0

        lax.fori_loop(0, R // 8, rows_step, 0)

    VM = pl.BlockSpec(memory_space=pltpu.VMEM)
    ncopy = sum(levels for parts in layout for _, _, _, levels, _ in parts) * H
    return pl.pallas_call(
        kernel,
        out_shape=[sds(nz, R, C)] * 3 + [sds(nz, 2, C)] + [sds(R, wide)] * 2,
        in_specs=[VM] * 6 + [ANY] * (len(flat) + len(after)),
        out_specs=[VM] * 6,
        scratch_shapes=[
            pltpu.VMEM((nz, R, C), f32),
            pltpu.VMEM((nz, R, C), f32),
            pltpu.VMEM((G, max(8, 2 * L), C), f32),
            pltpu.SemaphoreType.DMA((ncopy,)),
        ],
        compiler_params=WHOLE,
        cost_estimate=cost(24 * nz * R * C, 60 * nz * R * C),
    )(*planes, *rims, *flat, *after)


def lifted(geo, rim, west, east, after):
    nz, R, C = geo.shape
    deep = 4 if nz % 4 == 0 else 1

    def kernel(geo_ref, rim_ref, west_ref, east_ref, *refs):
        out_ref = refs[-1]
        lane = lax.broadcasted_iota(jnp.int32, (R, C), 1)
        row = lax.broadcasted_iota(jnp.int32, (R, C), 0)
        level = lax.broadcasted_iota(jnp.int32, west_ref.shape, 1)
        for d in range(deep):
            here = level == pl.program_id(0) * deep + d
            column = lambda ref: jnp.sum(jnp.where(here, ref[...], 0.0), axis=1, keepdims=True)
            g = geo_ref[d]
            north = jnp.where(row == 0, rim_ref[d, 0:1, :], pltpu.roll(g, 1, 0))
            south = jnp.where(row == R - 1, rim_ref[d, 1:2, :], pltpu.roll(g, R - 1, 0))
            left = jnp.where(lane == 0, column(west_ref), pltpu.roll(g, 1, 1))
            right = jnp.where(lane == C - 1, column(east_ref), pltpu.roll(g, C - 1, 1))
            out_ref[d] = lift_rate * (south + north + right + left - 4.0 * g)

    block = lambda *shape: pl.BlockSpec((deep, *shape), lambda k: (k, 0, 0))
    side = pl.BlockSpec(west.shape, lambda k: (0, 0))
    return [
        pl.pallas_call(
            kernel,
            out_shape=sds(nz, R, C),
            grid=(nz // deep,),
            in_specs=[block(R, C), block(2, C), side, side] + [ANY] * len(after),
            out_specs=block(R, C),
            compiler_params=WHOLE,
            cost_estimate=cost(8 * nz * R * C, 8 * nz * R * C),
        )(geo, rim, west, east, *after)
    ]


def smoothed(wind, before, behind, after):
    L, RS, Y = wind.shape

    def kernel(wind_ref, before_ref, behind_ref, *refs):
        out_ref = refs[-1]
        lane = lax.broadcasted_iota(jnp.int32, (RS, Y), 1)
        row = lax.broadcasted_iota(jnp.int32, (RS, Y), 0)
        w = wind_ref[0]
        north = jnp.where(row == 0, before_ref[0], pltpu.roll(w, 1, 0))
        south = jnp.where(row == RS - 1, behind_ref[0], pltpu.roll(w, RS - 1, 0))
        left = jnp.where(lane == 0, 0.0, pltpu.roll(w, 1, 1))
        right = jnp.where(lane == Y - 1, 0.0, pltpu.roll(w, Y - 1, 1))
        out_ref[0] = w + smooth_rate * (south + north + right + left - 4.0 * w)

    block = lambda rows: pl.BlockSpec((1, rows, Y), lambda k: (k, 0, 0))
    return [
        pl.pallas_call(
            kernel,
            out_shape=sds(L, RS, Y),
            grid=(L,),
            in_specs=[block(RS), block(1), block(1)] + [ANY] * len(after),
            out_specs=block(RS),
            compiler_params=WHOLE,
            cost_estimate=cost(8 * L * RS * Y, 8 * L * RS * Y),
        )(wind, before, behind, *after)
    ]


def substitute(pieces, lift, couple, inv, wind, r0, rows, G, H, L, R, C):
    nz = G * L
    nb = G // H
    tall = 8
    held = [] if wind is None else [wind]
    pieces = [p.reshape(nb * L, rows, C) for p in pieces]

    def kernel(lift_ref, couple_ref, inv_ref, *refs):
        ins = refs[:H]
        out, fo, li, co, iv, sem, sem_out = refs[H + len(held) :]
        i = lax.axis_index("gx")

        def loads(b):
            part = pl.ds(pl.multiple_of(b * tall, tall), tall)
            where = pl.ds(pl.multiple_of(r0 + b * tall, tall), tall)
            copies = []
            for src, dst in ((lift_ref, li), (couple_ref, co), (inv_ref, iv)):
                copies.append(
                    pltpu.make_async_copy(src.at[:, where, :], dst.at[:, part, :], sem.at[b, len(copies)])
                )
            for k in range(G):
                s = lax.bitwise_xor(i, k)
                copies.append(
                    pltpu.make_async_copy(
                        ins[k // nb].at[pl.ds(k % nb * L, L), part, :],
                        fo.at[pl.ds(s * L, L), part, :],
                        sem.at[b, len(copies)],
                    )
                )
            return copies

        def store(b):
            part = pl.ds(pl.multiple_of(b * tall, tall), tall)
            where = pl.ds(pl.multiple_of(r0 + b * tall, tall), tall)
            return pltpu.make_async_copy(li.at[:, part, :], out.at[:, where, :], sem_out.at[b])

        def begin(b, _):
            for c in loads(b):
                c.start()
            return 0

        def sweep(b, _):
            for c in loads(b):
                c.wait()
            part = pl.ds(pl.multiple_of(b * tall, tall), tall)
            value = jnp.zeros((tall, C), f32)
            for k in range(nz):
                force = fo[k, part, :] + li[k, part, :]
                if k:
                    force = force + co[k - 1, part, :] * value
                value = force * iv[k, part, :]
                li[k, part, :] = value
            for k in range(nz - 2, -1, -1):
                value = li[k, part, :] + (co[k, part, :] * iv[k, part, :]) * value
                li[k, part, :] = value
            store(b).start()
            return 0

        def finish(b, _):
            store(b).wait()
            return 0

        for stage in (begin, sweep, finish):
            lax.fori_loop(0, rows // tall, stage, 0)

    return pl.pallas_call(
        kernel,
        out_shape=sds(nz, R, C),
        in_specs=[ANY] * (3 + H + len(held)),
        out_specs=ANY,
        scratch_shapes=[pltpu.VMEM((nz, rows, C), f32)] * 4
        + [
            pltpu.SemaphoreType.DMA((rows // tall, G + 3)),
            pltpu.SemaphoreType.DMA((rows // tall,)),
        ],
        input_output_aliases={3 + H: 0} if held else {},
        compiler_params=WHOLE,
        cost_estimate=cost(20 * nz * rows * C, 8 * nz * rows * C),
    )(lift, couple, inv, *pieces, *held)


def on_device(theta, pressure, vertical_wind, terrain, column_mass, land_mask, pbl_top):
    G, H = lax.axis_size("gx"), lax.axis_size("gy")
    nb = G // H
    L, RS, Y = theta.shape
    R, C = RS // nb, Y // H
    slab = lambda a: a.reshape(a.shape[0], nb, -1, Y)
    after = []

    def step(kernel, *args):
        out = kernel(*args)
        after[:] = [out[0]]
        return out

    def send_to(x, ds, dr):
        return moved(x, G, H, ds, dr)

    def beside(x, axis, up):
        n = lax.axis_size(axis)
        pairs = [(i, i + 1) if up else (i + 1, i) for i in range(n - 1)]
        return lax.ppermute(x, axis, pairs)

    def family(a):
        return [slab(a)] + [slab(send_to(a, e, 0)) for e in range(1, nb)]

    def cut(parts, far=1):
        pieces = step(split_slab, parts, list(after), H, C, far)
        out = [pieces[0]] + [send_to(pieces[m], 0, m) for m in range(1, H)]
        for e in range(1, far):
            out += [send_to(pieces[e * H + m], e, m) for m in range(H)]
        return [out[e * H : e * H + H] for e in range(far)]

    def send(pieces, behind_of=()):
        pieces = step(regroup, pieces, [*after, *behind_of], H, nb)
        out = [pieces[0]] + [None] * (H - 1)
        for q in partners(H):
            out[q] = send_to(pieces[q], q * nb, 0)
        return out

    def later(*x):
        return lax.optimization_barrier((*x, *after))[: len(x)]

    full = (0, R)
    th = family(theta)
    own, rest, every = [0], list(range(1, nb)), list(range(nb))
    layout = []

    def chunk(*entries):
        parts, rows, off = [], [], 0
        for what, distances, lv0, lv1 in entries:
            if lv1 <= lv0:
                continue
            members = pr if what else th
            parts.append(([members[e] for e in distances], (lv0, lv1), full))
            for e in distances:
                rows.append((what, e, lv0, lv1 - lv0, off))
                off += (lv1 - lv0) * R
        layout.append(rows)
        return cut(parts)

    half = max(1, L // 2)
    first = chunk((0, own, 0, 1))
    second = chunk((0, rest, 0, 1), (0, own, 1, min(2, L)))
    pr = family(later(pressure)[0])
    lead = [send(first)]
    third = chunk((0, rest, 1, min(2, L)), (0, every, 2, L - 1), (0, own, max(2, L - 1), L))
    lead.append(send(second))
    grown = chunk((0, rest, max(2, L - 1), L), (1, every, 0, half))

    sources = later(theta, pressure, vertical_wind)
    before = beside(jnp.stack([a[:, RS - 1 :] for a in sources]), "gy", True)
    behind = beside(jnp.stack([a[:, :1] for a in sources]), "gy", False)

    lead.append(send(third))
    lead.append(send(grown))

    blown = step(smoothed, vertical_wind, before[2], behind[2], list(after))[0]
    safe = lambda p: jnp.where(p > 0, p, 1.0)
    theta, pressure, before, behind = later(theta, pressure, before, behind)
    rims = []
    for b in range(nb):
        lines = []
        for lo, src in ((b * R - 1, before), ((b + 1) * R, behind)):
            if 0 <= lo < RS:
                t, p = theta[:, lo, :], pressure[:, lo, :]
            else:
                t, p = src[0, :, 0, :], safe(src[1, :, 0, :])
            lines.append(states(t, p)[0])
        rims.append(jnp.stack(lines, 1).reshape(2 * L, Y))
    tall = -(-2 * L // 8) * 8
    rim = jnp.pad(jnp.stack(rims), ((0, 0), (0, tall - 2 * L), (0, 0))).reshape(1, nb * tall, Y)
    rim, blown = family(rim), family(blown)

    fourth = cut([(pr, (half, L), full), (rim, (0, 1), (0, tall))])
    part, last = max(8, R // 4 // 8 * 8), max(8, R // 4 // 8 * 8)
    marks = sorted({0, min(part, R), max(R - last, min(part, R)), R})
    rows_cut = list(zip(marks[:-1], marks[1:]))
    cuts = [cut([(blown, (0, L), rows_cut[0])])]
    lead.append(send(fourth))
    plane_rim = lambda a: jnp.concatenate([beside(a[-1:], "gx", True), beside(a[:1], "gx", False)], 0)
    rim_planes = [plane_rim(a) for a in later(terrain, column_mass)]
    n = L - half
    layout.append(
        [(1, e, half, n, e * n * R) for e in range(nb)]
        + [(2, e, 0, 1, nb * n * R + e * tall) for e in range(nb)]
    )
    cuts += [cut([(blown, (0, L), rows)]) for rows in rows_cut[1:]]
    winds = [send(cuts[0], lead[-2][1:])]
    winds += [send(pieces, lead[-1][1:]) for pieces in cuts[1:-1]]

    planes = (terrain, column_mass, land_mask, pbl_top)
    geo, couple, inv, rim_geo, west, east = step(
        coefficients, lead, layout, planes, rim_planes, list(after), G, H, L, R, C
    )
    west, east = beside(east, "gy", True), beside(west, "gy", False)
    winds += [send(pieces) for pieces in cuts[len(winds) :]]
    lift = step(lifted, geo, rim_geo, west, east, list(after))[0]

    wind = None
    for (r0, r1), pieces in zip(rows_cut, winds):
        wind = substitute(pieces, lift, couple, inv, wind, r0, r1 - r0, G, H, L, R, C)
    return wind, geo


def solution(mesh):
    placed = (P("gx", "gy", None),) * 3 + (P("gx", "gy"),) * 4

    fn = jax.shard_map(
        on_device,
        mesh=mesh,
        in_specs=placed,
        out_specs=(P(None, "gx", "gy"), P(None, "gx", "gy")),
        check_vma=False,
    )

    def traced(*args):
        jax.eval_shape(fn, *args)
        return fn(*args)

    return traced
```
